32 devices in a mesh: bfly: 32 (over z, y, x, core).
Axes of the slice: x: 2, y: 2, z: 4, core: 2. Of those that a mesh axis runs over, the one named last changes fastest.
Arguments:
- coeffs: float32 [32, 384, 1024], P('bfly'), may hold values from -6 to 6
- transfers: float32 [32, 8, 2, 384, 384], P('bfly'), may hold values from -0.21875 to 0.21875
Outputs:
- result: float32 [32, 384, 1024], P('bfly')
The draws below stay inside these ranges and needn't reach their ends.
All inputs are finite; a program needn't handle non-finite values.
Results may differ from the reference program's by a relative error of at most 0.00014.
Values sent between devices are 32-bit elements; how exact they have to be, the bound alone decides.
A program may use at most 64 MiB of HBM per device.

```python
import jax
import jax.numpy as jnp
from jax import lax

RANK = 384
COLS = 1024
LEVELS = 8
NODES = 32
N_BFLY = 32


def level_of(key, extent, shards, low, high):
    gain = 1.0
    for position, blocks in shards:
        draws = jax.random.uniform(jax.random.fold_in(jax.random.fold_in(key, 6), position), (blocks,), jnp.float32, low / len(shards), high / len(shards))
        gain = gain * jnp.repeat(jnp.exp(draws), extent[position] // blocks).reshape((-1,) + (1,) * (len(extent) - 1 - position))
    return gain


def scatter_about(key, shape, width, most, cuts=(), kind=jnp.bfloat16):
    values = jax.random.normal(key, shape, jnp.float32) * width
    if len(cuts) > 0:
        values = level_of(key, shape, cuts, -0.22, 0.18) * values
    return jnp.clip(values, min=-most, max=most).astype(kind)


def setup_inputs(seed: int = 0) -> dict:
    key_list = jax.random.split(jax.random.key(seed), 3)
    coeffs = scatter_about(key_list[0], (NODES, RANK, COLS), 1.0, 6.0, ((0, 32),), jnp.float32)
    transfers = scatter_about(key_list[1], (NODES, LEVELS, 2, RANK, RANK), (2 * RANK) ** -0.5, 0.21875, ((0, 32),), jnp.float32)
    return {"coeffs": coeffs, "transfers": transfers}


def reference(coeffs, transfers):
    bit_count = N_BFLY.bit_length() - 1
    node_ids = jnp.arange(N_BFLY, dtype=jnp.int32)
    state = coeffs
    for depth_level in range(LEVELS):
        bit_value = 1 << (depth_level % bit_count)
        partner = jnp.bitwise_xor(node_ids, bit_value).astype(jnp.int32)
        own_term = jnp.einsum("nij,njc->nic", transfers[:, depth_level, 0], state, precision=lax.Precision.HIGHEST)
        sent_term = jnp.einsum("nij,njc->nic", transfers[:, depth_level, 1], state, precision=lax.Precision.HIGHEST)
        state = own_term + sent_term[partner]
    return state
```

```python
import functools

import jax
import jax.numpy as jnp
from jax import lax
from jax.experimental import pallas as pl
from jax.experimental.pallas import tpu as pltpu
from jax.sharding import PartitionSpec as P

LANES = 128
CHUNK = 64
RAMP = (32, 32)
DUE = (0.0, 2.1, 6.5, 11.9, 17.4, 24.8, 25.6, 33.5, 44.4)
PACE = 0.066
GROUP = 9


def chunk_runs(cols):
    body = cols - 2 * sum(RAMP)
    sizes = (CHUNK,) * (cols // CHUNK)
    if body > 0 and body % CHUNK == 0:
        sizes = RAMP + (CHUNK,) * (body // CHUNK) + RAMP[::-1]
    runs = []
    for k, size in enumerate(sizes):
        if not runs or runs[-1][2] != size:
            runs.append((k, sum(sizes[:k]), size))
    return runs, sizes


def task_order(sizes, levels):
    dues = [DUE[i] if i < len(DUE) else DUE[-1] + 6.0 * (i - len(DUE) + 1) for i in range(levels + 1)]
    steps = sorted(
        (sum(sizes[:k]) * PACE + dues[level], -level, level, k)
        for k in range(len(sizes)) for level in range(levels + 1)
    )
    return [(level, k) for _, _, level, k in steps]


def kernel(axis, bits, levels, coeffs, transfers, out, own, sent, got, raw, mats, turn, back,
           in_sem, raw_sem, out_sem, send_sem, recv_sem):
    me = lax.axis_index(axis)
    cols, rank = own.shape
    blocks = cols // LANES
    runs, sizes = chunk_runs(cols)
    order = task_order(sizes, levels)
    base = max(levels + 1, len(sizes))

    def peer(level):
        step = lax.shift_left(jnp.int32(1), lax.rem(jnp.int32(level), jnp.int32(bits)))
        return me + step * (1 - 2 * lax.rem(lax.div(me, step), jnp.int32(2)))

    def lanes(b):
        return pl.ds(pl.multiple_of(b * LANES, LANES), LANES)

    def load_block(b):
        return pltpu.make_async_copy(coeffs.at[0, :, lanes(b)], turn.at[b], in_sem.at[b])

    def load_level(level):
        return pltpu.make_async_copy(transfers.at[0, level], raw.at[level], raw_sem.at[level])

    def store_block(b):
        return pltpu.make_async_copy(back.at[b], out.at[0, :, lanes(b)], out_sem.at[b])

    def exchange(level, k, rows):
        return pltpu.make_async_remote_copy(
            src_ref=sent.at[level, rows],
            dst_ref=got.at[level + 1, rows],
            send_sem=send_sem.at[level],
            recv_sem=recv_sem.at[level, k],
            device_id=(peer(level),),
            device_id_type=pl.DeviceIdType.MESH,
        )

    barrier = pltpu.get_barrier_semaphore()
    for bit in range(min(bits, levels)):
        pl.semaphore_signal(barrier, inc=1, device_id=(peer(bit),),
                            device_id_type=pl.DeviceIdType.MESH)

    load_block(0).start()
    for level in range(levels):
        load_level(level).start()
        if level == 0:
            for b in range(1, blocks):
                load_block(b).start()

    def prepare(level):
        load_level(level).wait()
        for side in range(2):
            full = raw[level, side].T
            high = full.astype(jnp.bfloat16)
            low = (full - high.astype(jnp.float32)).astype(jnp.bfloat16)
            mats[level, 0:rank, side * rank:(side + 1) * rank] = high
            mats[level, rank:2 * rank, side * rank:(side + 1) * rank] = low

    def turn_block(b):
        load_block(b).wait()
        rows = pl.ds(pl.multiple_of(b * LANES, LANES), LANES)
        own[rows] = turn[b].T
        got[0, rows] = jnp.zeros((LANES, rank), jnp.float32)

    def apply(size, level, k, row):
        rows = pl.ds(pl.multiple_of(row, 16), size)

        @pl.when(k == 0)
        def _():
            prepare(level)

        @pl.when((level == 0) & (lax.rem(row, LANES) == 0))
        def _():
            turn_block(lax.div(row, LANES))

        @pl.when(level > 0)
        def _():
            exchange(level - 1, k, rows).wait_recv()

        state = own[rows] + got[level, rows]
        high = state.astype(jnp.bfloat16)
        low = (state - high.astype(jnp.float32)).astype(jnp.bfloat16)
        both = jnp.dot(jnp.concatenate([high, low], axis=0), mats[level, 0:rank],
                       preferred_element_type=jnp.float32)
        rest = jnp.dot(high, mats[level, rank:2 * rank], preferred_element_type=jnp.float32)
        terms = both[:size] + both[size:] + rest
        sent[level, rows] = terms[:, rank:]
        exchange(level, k, rows).start()
        own[rows] = terms[:, :rank]

    def finish(size, k, row):
        rows = pl.ds(pl.multiple_of(row, 16), size)
        exchange(levels - 1, k, rows).wait_recv()
        own[rows] = own[rows] + got[levels, rows]

        @pl.when(lax.rem(row + size, LANES) == 0)
        def _():
            b = lax.div(row, LANES)
            back[b] = own[pl.ds(pl.multiple_of(b * LANES, LANES), LANES)].T
            store_block(b).start()

    pl.semaphore_wait(barrier, min(bits, levels))

    pack = 1
    while (base * base) ** (pack + 1) < 2**31:
        pack += 1
    digits = [level * base + k for level, k in order]
    words = [
        sum(d * (base * base) ** i for i, d in enumerate(digits[n:n + pack]))
        for n in range(0, len(digits), pack)
    ]
    per = GROUP // pack
    groups = pl.cdiv(len(words), per)
    words += [0] * (groups * per - len(words))

    def group(g, carry):
        held = []
        for n in range(per):
            word = jnp.int32(words[n])
            for other in range(1, groups):
                word = jnp.where(g == other, jnp.int32(words[other * per + n]), word)
            held.append(word)

        def step(j, carry):
            word = held[0]
            for n in range(1, per):
                word = jnp.where(j >= n * pack, held[n], word)
            place = lax.rem(j, jnp.int32(pack))
            for i in range(1, pack):
                word = jnp.where(place >= i, lax.div(word, jnp.int32(base * base)), word)
            word = lax.rem(word, jnp.int32(base * base))
            level = lax.div(word, jnp.int32(base))
            k = lax.rem(word, jnp.int32(base))
            row = jnp.int32(0)
            for first, column, size in runs:
                row = jnp.where(k >= first, column + (k - first) * size, row)

            for n, size in enumerate(sorted(set(sizes))):
                among = False
                for (first, _, its), last in zip(runs, [r[0] for r in runs[1:]] + [len(sizes)]):
                    if its == size:
                        among = among | ((k >= first) & (k < last))

                @pl.when(among & (level < levels))
                def _():
                    apply(size, level, k, row)

                @pl.when(among & (level == levels))
                def _():
                    finish(size, k, row)
            return carry

        count = jnp.minimum(per * pack, len(order) - g * per * pack)
        return lax.fori_loop(0, count, step, carry)

    lax.fori_loop(0, groups, group, 0)

    for level in range(levels):
        exchange(level, 0, pl.ds(0, cols)).wait_send()

    for b in range(blocks):
        store_block(b).wait()


def on_device(coeffs, transfers):
    bits = lax.axis_size("bfly").bit_length() - 1
    _, rank, cols = coeffs.shape
    levels = transfers.shape[1]
    _, sizes = chunk_runs(cols)
    blocks = cols // LANES
    f32, bf16 = jnp.float32, jnp.bfloat16
    return pl.pallas_call(
        functools.partial(kernel, "bfly", bits, levels),
        out_shape=jax.ShapeDtypeStruct(coeffs.shape, f32),
        in_specs=[pl.BlockSpec(memory_space=pl.ANY)] * 2,
        out_specs=pl.BlockSpec(memory_space=pl.ANY),
        scratch_shapes=[
            pltpu.VMEM((cols, rank), f32),
            pltpu.VMEM((levels, cols, rank), f32),
            pltpu.VMEM((levels + 1, cols, rank), f32),
            pltpu.VMEM((levels, 2, rank, rank), f32),
            pltpu.VMEM((levels, 2 * rank, 2 * rank), bf16),
            pltpu.VMEM((blocks, rank, LANES), f32),
            pltpu.VMEM((blocks, rank, LANES), f32),
            pltpu.SemaphoreType.DMA((blocks,)),
            pltpu.SemaphoreType.DMA((levels,)),
            pltpu.SemaphoreType.DMA((blocks,)),
            pltpu.SemaphoreType.DMA((levels,)),
            pltpu.SemaphoreType.DMA((levels, len(sizes))),
        ],
        compiler_params=pltpu.CompilerParams(
            collective_id=0, has_side_effects=True, vmem_limit_bytes=60 * 2**20
        ),
        name="butterfly",
    )(coeffs, transfers)


def solution(mesh):
    return jax.shard_map(
        on_device,
        mesh=mesh,
        in_specs=(P("bfly", None, None), P("bfly", None, None, None, None)),
        out_specs=P("bfly", None, None),
        check_vma=False,
    )
```

```python
import functools

import jax
import jax.numpy as jnp
from jax import lax
from jax.experimental import pallas as pl
from jax.experimental.pallas import tpu as pltpu
from jax.sharding import PartitionSpec as P

LANES = 128
CHUNK = 64
RAMP = (32, 32)
DUE = (0.0, 4.3, 9.0, 13.5, 18.0, 25.0, 27.5, 33.5, 42.0)
PACE = 0.066
AHEAD = 0.066
TURN = 4
GROUP = 9
PREPARE_AFTER = 2


def chunk_runs(cols):
    body = cols - 2 * sum(RAMP)
    sizes = (CHUNK,) * (cols // CHUNK)
    if body > 0 and body % CHUNK == 0:
        sizes = RAMP + (CHUNK,) * (body // CHUNK) + RAMP[::-1]
    runs = []
    for k, size in enumerate(sizes):
        if not runs or runs[-1][2] != size:
            runs.append((k, sum(sizes[:k]), size))
    return runs, sizes


def task_order(sizes, levels):
    dues = [DUE[i] if i < len(DUE) else DUE[-1] + 6.0 * (i - len(DUE) + 1) for i in range(levels + 1)]
    firsts = [sum(sizes[:k]) for k in range(len(sizes))]
    steps = [
        (firsts[k] * (AHEAD if level < TURN else PACE) + dues[level], -level, level, k)
        for k in range(len(sizes)) for level in range(levels + 1)
    ]
    order, turned = [], {0}
    for _, _, level, k in sorted(steps):
        block = firsts[k] // LANES
        if level == 0 and block not in turned:
            turned.add(block)
            order.append((levels + 2, block))
        order.append((level, k))
    for level in range(1, levels):
        at = order.index((level - 1, min(PREPARE_AFTER, len(sizes) - 1)))
        order.insert(min(at + 1, order.index((level, 0))), (levels + 1, level))
    return order


def ring_size(order, sizes, levels):
    place = {task: i for i, task in enumerate(order)}
    for ring in range(1, len(sizes)):
        if all(
            any(
                place[level + 1, k] < place[level, j] and place[level + 1, j] < place[level, k + ring]
                for j in range(len(sizes))
            )
            for level in range(levels) for k in range(len(sizes) - ring)
        ):
            return ring
    return len(sizes)


def kernel(axis, bits, levels, coeffs, transfers, out, own, sent, got, raw, mats, turn,
           in_sem, raw_sem, send_sem, recv_sem):
    me = lax.axis_index(axis)
    cols, rank = own.shape
    blocks = cols // LANES
    runs, sizes = chunk_runs(cols)
    order = task_order(sizes, levels)
    base = max(levels + 3, len(sizes))
    ring = ring_size(order, sizes, levels)

    def peer(level):
        step = lax.shift_left(jnp.int32(1), lax.rem(jnp.int32(level), jnp.int32(bits)))
        return me + step * (1 - 2 * lax.rem(lax.div(me, step), jnp.int32(2)))

    def lanes(b):
        return pl.ds(pl.multiple_of(b * LANES, LANES), LANES)

    def load_columns(first, count, sem):
        columns = (slice(None), pl.ds(first, count))
        return pltpu.make_async_copy(coeffs.at[(0, *columns)], turn.at[columns], in_sem.at[sem])

    def load_side(side):
        return pltpu.make_async_copy(transfers.at[0, 0, side], raw.at[0, side], raw_sem.at[side])

    def load_levels(first, count, sem):
        those = pl.ds(first, count)
        return pltpu.make_async_copy(transfers.at[0, those], raw.at[those], raw_sem.at[sem])

    loads = [load_columns(0, LANES, 0)]
    if blocks > 1:
        loads.append(load_columns(LANES, cols - LANES, 1))
    later = [load_levels(1, 1, 2), load_levels(2, levels - 2, 3)]

    def exchange(level, k, rows):
        return pltpu.make_async_remote_copy(
            src_ref=sent.at[level, rows],
            dst_ref=got.at[level + 1, rows],
            send_sem=send_sem.at[0],
            recv_sem=recv_sem.at[level * ring + lax.rem(k, ring)],
            device_id=(peer(level),),
            device_id_type=pl.DeviceIdType.MESH,
        )

    barrier = pltpu.get_barrier_semaphore()
    for bit in range(min(bits, levels)):
        pl.semaphore_signal(barrier, inc=1, device_id=(peer(bit),),
                            device_id_type=pl.DeviceIdType.MESH)

    load_side(1).start()
    loads[0].start()
    load_side(0).start()
    later[0].start()
    for load in loads[1:]:
        load.start()
    later[1].start()

    def prepare_side(level, side):
        full = raw[level, side].T
        high = full.astype(jnp.bfloat16)
        low = (full - high.astype(jnp.float32)).astype(jnp.bfloat16)
        mats[level, 0:rank, side * rank:(side + 1) * rank] = high
        mats[level, rank:2 * rank, side * rank:(side + 1) * rank] = low

    def prepare(level):
        for n, load in enumerate(later):
            @pl.when(level == n + 1)
            def _():
                load.wait()

        for side in range(2):
            prepare_side(level, side)

    def turn_block(b):
        rows = pl.ds(pl.multiple_of(b * LANES, LANES), LANES)
        own[rows] = turn[:, rows].T
        got[0, rows] = jnp.zeros((LANES, rank), jnp.float32)

    def apply(size, level, k, row):
        rows = pl.ds(pl.multiple_of(row, 16), size)

        @pl.when(level > 0)
        def _():
            exchange(level - 1, k, rows).wait_recv()

        state = own[rows] + got[level, rows]
        high = state.astype(jnp.bfloat16)
        low = (state - high.astype(jnp.float32)).astype(jnp.bfloat16)
        both = jnp.dot(jnp.concatenate([high, low], axis=0), mats[level, 0:rank],
                       preferred_element_type=jnp.float32)
        rest = jnp.dot(high, mats[level, rank:2 * rank], preferred_element_type=jnp.float32)
        terms = both[:size] + both[size:] + rest
        sent[level, rows] = terms[:, rank:]
        exchange(level, k, rows).start()
        own[rows] = terms[:, :rank]

    def finish(size, k, row):
        rows = pl.ds(pl.multiple_of(row, 16), size)
        exchange(levels - 1, k, rows).wait_recv()
        own[rows] = own[rows] + got[levels, rows]

        @pl.when(lax.rem(row + size, LANES) == 0)
        def _():
            b = lax.div(row, LANES)
            out[0, :, lanes(b)] = own[pl.ds(pl.multiple_of(b * LANES, LANES), LANES)].T

    load_side(1).wait()
    prepare_side(0, 1)
    loads[0].wait()
    turn_block(0)
    load_side(0).wait()
    prepare_side(0, 0)
    pl.semaphore_wait(barrier, min(bits, levels))

    pack = 1
    while (base * base) ** (pack + 1) < 2**31:
        pack += 1
    digits = [level * base + k for level, k in order]
    words = [
        sum(d * (base * base) ** i for i, d in enumerate(digits[n:n + pack]))
        for n in range(0, len(digits), pack)
    ]
    per = GROUP // pack
    groups = pl.cdiv(len(words), per)
    words += [0] * (groups * per - len(words))

    def group(g, carry):
        held = []
        for n in range(per):
            word = jnp.int32(words[n])
            for other in range(1, groups):
                word = jnp.where(g == other, jnp.int32(words[other * per + n]), word)
            held.append(word)

        def step(j, carry):
            word = held[0]
            for n in range(1, per):
                word = jnp.where(j >= n * pack, held[n], word)
            place = lax.rem(j, jnp.int32(pack))
            for i in range(1, pack):
                word = jnp.where(place >= i, lax.div(word, jnp.int32(base * base)), word)
            word = lax.rem(word, jnp.int32(base * base))
            level = lax.div(word, jnp.int32(base))
            k = lax.rem(word, jnp.int32(base))
            row = jnp.int32(0)
            for first, column, size in runs:
                row = jnp.where(k >= first, column + (k - first) * size, row)

            for n, size in enumerate(sorted(set(sizes))):
                among = False
                for (first, _, its), last in zip(runs, [r[0] for r in runs[1:]] + [len(sizes)]):
                    if its == size:
                        among = among | ((k >= first) & (k < last))

                @pl.when(among & (level < levels))
                def _():
                    apply(size, level, k, row)

                @pl.when(among & (level == levels))
                def _():
                    finish(size, k, row)

            @pl.when(level == levels + 1)
            def _():
                prepare(k)

            @pl.when(level == levels + 2)
            def _():
                @pl.when(k == 1)
                def _():
                    loads[1].wait()

                turn_block(k)
            return carry

        count = jnp.minimum(per * pack, len(order) - g * per * pack)
        return lax.fori_loop(0, count, step, carry)

    lax.fori_loop(0, groups, group, 0)

    pltpu.make_async_remote_copy(
        src_ref=sent, dst_ref=got.at[pl.ds(1, levels)], send_sem=send_sem.at[0], recv_sem=recv_sem.at[0],
        device_id=(peer(0),), device_id_type=pl.DeviceIdType.MESH,
    ).wait_send()


def on_device(coeffs, transfers):
    bits = lax.axis_size("bfly").bit_length() - 1
    _, rank, cols = coeffs.shape
    levels = transfers.shape[1]
    _, sizes = chunk_runs(cols)
    f32, bf16 = jnp.float32, jnp.bfloat16
    return pl.pallas_call(
        functools.partial(kernel, "bfly", bits, levels),
        out_shape=pltpu.VMEM(coeffs.shape, f32),
        in_specs=[pl.BlockSpec(memory_space=pl.ANY)] * 2,
        out_specs=pl.BlockSpec(memory_space=pltpu.VMEM),
        scratch_shapes=[
            pltpu.VMEM((cols, rank), f32),
            pltpu.VMEM((levels, cols, rank), f32),
            pltpu.VMEM((levels + 1, cols, rank), f32),
            pltpu.VMEM((levels, 2, rank, rank), f32),
            pltpu.VMEM((levels, 2 * rank, 2 * rank), bf16),
            pltpu.VMEM((rank, cols), f32),
            pltpu.SemaphoreType.DMA((2,)),
            pltpu.SemaphoreType.DMA((4,)),
            pltpu.SemaphoreType.DMA((1,)),
            pltpu.SemaphoreType.DMA((levels * ring_size(task_order(sizes, levels), sizes, levels),)),
        ],
        compiler_params=pltpu.CompilerParams(
            collective_id=0, has_side_effects=True, vmem_limit_bytes=52 * 2**20
        ),
        name="butterfly",
    )(coeffs, transfers)


def solution(mesh):
    return jax.shard_map(
        on_device,
        mesh=mesh,
        in_specs=(P("bfly", None, None), P("bfly", None, None, None, None)),
        out_specs=P("bfly", None, None),
        check_vma=False,
    )
```

```python
import functools

import jax
import jax.numpy as jnp
from jax import lax
from jax.experimental import pallas as pl
from jax.experimental.pallas import tpu as pltpu
from jax.sharding import PartitionSpec as P

LANES = 128
CHUNK = 64
RAMP = (32, 32, 32, 32,)
DUE = (0.00, 3.90, 11.33, 18.99, 26.21, 37.55, 40.12, 48.33, 59.96)
PACE = 0.0716
AHEAD = 0.0700
TURN = 4
GROUP = 9
PREPARE_AFTER = 4


def chunk_runs(cols):
    body = cols - 2 * sum(RAMP)
    sizes = (CHUNK,) * (cols // CHUNK)
    if body > 0 and body % CHUNK == 0:
        sizes = RAMP + (CHUNK,) * (body // CHUNK) + RAMP[::-1]
    runs = []
    for k, size in enumerate(sizes):
        if not runs or runs[-1][2] != size:
            runs.append((k, sum(sizes[:k]), size))
    return runs, sizes


def task_order(sizes, levels):
    dues = [DUE[i] if i < len(DUE) else DUE[-1] + 6.0 * (i - len(DUE) + 1) for i in range(levels + 1)]
    firsts = [sum(sizes[:k]) for k in range(len(sizes))]
    steps = [
        (firsts[k] * (AHEAD if level < TURN else PACE) + dues[level], -level, level, k)
        for k in range(len(sizes)) for level in range(levels + 1)
    ]
    order, turned = [], {0}
    for _, _, level, k in sorted(steps):
        block = firsts[k] // LANES
        if level == 0 and block not in turned:
            turned.add(block)
            order.append((levels + 2, block))
        order.append((level, k))
    for level in range(1, levels):
        at = order.index((level - 1, min(PREPARE_AFTER if level > 1 else 0, len(sizes) - 1)))
        order.insert(min(at + 1, order.index((level, 0))), (levels + 1, level))
    return order


def modulo(x, n):
    return lax.bitwise_and(x, jnp.int32(n - 1)) if n & (n - 1) == 0 else lax.rem(x, jnp.int32(n))


def ring_size(order, sizes, levels):
    place = {task: i for i, task in enumerate(order)}
    for ring in range(1, len(sizes)):
        if all(
            any(
                place[level + 1, k] < place[level, j] and place[level + 1, j] < place[level, k + ring]
                for j in range(len(sizes))
            )
            for level in range(levels) for k in range(len(sizes) - ring)
        ):
            return 8 if ring in (5, 6, 7) else ring
    return len(sizes)


def kernel(axis, bits, levels, coeffs, transfers, out, own, sent, got, raw, mats, turn,
           in_sem, raw_sem, send_sem, recv_sem):
    me = lax.axis_index(axis)
    cols, rank = own.shape
    blocks = cols // LANES
    runs, sizes = chunk_runs(cols)
    order = task_order(sizes, levels)
    ring = ring_size(order, sizes, levels)

    def peer(level):
        bit = jnp.int32(level)
        for _ in range((levels - 1) // bits):
            bit = jnp.where(bit >= bits, bit - bits, bit)
        return lax.bitwise_xor(me, lax.shift_left(jnp.int32(1), bit))

    def lanes(b):
        return pl.ds(pl.multiple_of(b * LANES, LANES), LANES)

    def load_columns(first, count, sem):
        columns = (slice(None), pl.ds(first, count))
        return pltpu.make_async_copy(coeffs.at[(0, *columns)], turn.at[columns], in_sem.at[sem])

    def load_side(side):
        return pltpu.make_async_copy(transfers.at[0, 0, side], raw.at[0, side], raw_sem.at[side])

    def load_levels(first, count, sem):
        those = pl.ds(first, count)
        return pltpu.make_async_copy(transfers.at[0, those], raw.at[those], raw_sem.at[sem])

    loads = [load_columns(0, LANES, 0)]
    if blocks > 1:
        loads.append(load_columns(LANES, cols - LANES, 1))
    later = [load_levels(1, 1, 2), load_levels(2, levels - 2, 3)]

    def exchange(level, k, rows):
        return pltpu.make_async_remote_copy(
            src_ref=sent.at[level, rows],
            dst_ref=got.at[level + 1, rows],
            send_sem=send_sem.at[0],
            recv_sem=recv_sem.at[level * ring + modulo(k, ring)],
            device_id=(peer(level),),
            device_id_type=pl.DeviceIdType.MESH,
        )

    barrier = pltpu.get_barrier_semaphore()
    for bit in range(min(bits, levels)):
        pl.semaphore_signal(barrier, inc=1, device_id=(peer(bit),),
                            device_id_type=pl.DeviceIdType.MESH)

    load_side(1).start()
    loads[0].start()
    load_side(0).start()
    later[0].start()
    for load in loads[1:]:
        load.start()
    later[1].start()

    def prepare_side(level, side):
        full = raw[level, side].T
        high = full.astype(jnp.bfloat16)
        low = (full - high.astype(jnp.float32)).astype(jnp.bfloat16)
        mats[level, 0:rank, side * rank:(side + 1) * rank] = high
        mats[level, rank:2 * rank, side * rank:(side + 1) * rank] = low

    def prepare(level):
        for n, load in enumerate(later):
            @pl.when(level == n + 1)
            def _():
                load.wait()

        for side in range(2):
            prepare_side(level, side)

    def turn_block(b):
        rows = pl.ds(pl.multiple_of(b * LANES, LANES), LANES)
        own[rows] = turn[:, rows].T
        got[0, rows] = jnp.zeros((LANES, rank), jnp.float32)

    def products(state, level):
        size = state.shape[0]
        high = state.astype(jnp.bfloat16)
        low = (state - high.astype(jnp.float32)).astype(jnp.bfloat16)
        stack = jnp.concatenate([high, low], axis=0)

        def terms(first, count):
            columns = slice(first * rank, (first + count) * rank)
            both = jnp.dot(stack, mats[level, 0:rank, columns], preferred_element_type=jnp.float32)
            rest = jnp.dot(high, mats[level, rank:2 * rank, columns], preferred_element_type=jnp.float32)
            return both[:size] + both[size:] + rest

        return terms

    def apply(size, level, k, row):
        rows = pl.ds(pl.multiple_of(row, 16), size)

        @pl.when(level > 0)
        def _():
            exchange(level - 1, k, rows).wait_recv()

        terms = products(own[rows] + got[level, rows], level)
        if size < CHUNK:
            sent[level, rows] = terms(1, 1)
            exchange(level, k, rows).start()
            own[rows] = terms(0, 1)
        else:
            both = terms(0, 2)
            sent[level, rows] = both[:, rank:]
            exchange(level, k, rows).start()
            own[rows] = both[:, :rank]

    def finish(size, k, row):
        rows = pl.ds(pl.multiple_of(row, 16), size)
        exchange(levels - 1, k, rows).wait_recv()
        own[rows] = own[rows] + got[levels, rows]

        @pl.when(lax.rem(row + size, LANES) == 0)
        def _():
            b = lax.div(row, LANES)
            out[0, :, lanes(b)] = own[pl.ds(pl.multiple_of(b * LANES, LANES), LANES)].T

    load_side(1).wait()
    prepare_side(0, 1)
    loads[0].wait()
    turn_block(0)
    pl.semaphore_wait(barrier, min(bits, levels))

    rows = pl.ds(0, sizes[0])
    terms = products(own[rows], 0)
    sent[0, rows] = terms(1, 1)
    exchange(jnp.int32(0), jnp.int32(0), rows).start()
    load_side(0).wait()
    prepare_side(0, 0)
    own[rows] = terms(0, 1)

    width = max(levels + 2, len(sizes) - 1).bit_length()
    pack = 31 // (2 * width)
    digits = [(level << width) + k for level, k in order if (level, k) != (0, 0)]
    words = [
        sum(d << (2 * width * i) for i, d in enumerate(digits[n:n + pack]))
        for n in range(0, len(digits), pack)
    ]
    per = GROUP // pack
    groups = pl.cdiv(len(words), per)
    words += [0] * (groups * per - len(words))

    def group(g, carry):
        held = []
        for n in range(per):
            word = jnp.int32(words[n])
            for other in range(1, groups):
                word = jnp.where(g == other, jnp.int32(words[other * per + n]), word)
            held.append(word)

        def step(j, carry):
            word = held[0]
            for n in range(1, per):
                word = jnp.where(j >= n * pack, held[n], word)
            place = j
            for n in range(1, per):
                place = jnp.where(j >= n * pack, j - n * pack, place)
            word = lax.shift_right_logical(word, place * (2 * width))
            level = lax.bitwise_and(lax.shift_right_logical(word, jnp.int32(width)), jnp.int32(2**width - 1))
            k = lax.bitwise_and(word, jnp.int32(2**width - 1))
            row = jnp.int32(0)
            for first, column, size in runs:
                row = jnp.where(k >= first, column + (k - first) * size, row)

            def by_size(act):
                for size in sorted(set(sizes)):
                    among = False
                    for (first, _, its), last in zip(runs, [r[0] for r in runs[1:]] + [len(sizes)]):
                        if its == size:
                            among = among | ((k >= first) & (k < last))

                    @pl.when(among)
                    def _():
                        act(size)

            @pl.when(level < levels)
            def _():
                by_size(lambda size: apply(size, level, k, row))

            @pl.when(level == levels)
            def _():
                by_size(lambda size: finish(size, k, row))

            @pl.when(level == levels + 1)
            def _():
                prepare(k)

            @pl.when(level == levels + 2)
            def _():
                @pl.when(k == 1)
                def _():
                    loads[1].wait()

                turn_block(k)
            return carry

        count = jnp.minimum(per * pack, len(digits) - g * per * pack)
        return lax.fori_loop(0, count, step, carry)

    lax.fori_loop(0, groups, group, 0)

    pltpu.make_async_remote_copy(
        src_ref=sent, dst_ref=got.at[pl.ds(1, levels)], send_sem=send_sem.at[0], recv_sem=recv_sem.at[0],
        device_id=(peer(0),), device_id_type=pl.DeviceIdType.MESH,
    ).wait_send()


def on_device(coeffs, transfers):
    bits = lax.axis_size("bfly").bit_length() - 1
    _, rank, cols = coeffs.shape
    levels = transfers.shape[1]
    _, sizes = chunk_runs(cols)
    f32, bf16 = jnp.float32, jnp.bfloat16
    return pl.pallas_call(
        functools.partial(kernel, "bfly", bits, levels),
        out_shape=pltpu.VMEM(coeffs.shape, f32),
        in_specs=[pl.BlockSpec(memory_space=pl.ANY)] * 2,
        out_specs=pl.BlockSpec(memory_space=pltpu.VMEM),
        scratch_shapes=[
            pltpu.VMEM((cols, rank), f32),
            pltpu.VMEM((levels, cols, rank), f32),
            pltpu.VMEM((levels + 1, cols, rank), f32),
            pltpu.VMEM((levels, 2, rank, rank), f32),
            pltpu.VMEM((levels, 2 * rank, 2 * rank), bf16),
            pltpu.VMEM((rank, cols), f32),
            pltpu.SemaphoreType.DMA((2,)),
            pltpu.SemaphoreType.DMA((4,)),
            pltpu.SemaphoreType.DMA((1,)),
            pltpu.SemaphoreType.DMA((levels * ring_size(task_order(sizes, levels), sizes, levels),)),
        ],
        compiler_params=pltpu.CompilerParams(
            collective_id=0, has_side_effects=True, vmem_limit_bytes=52 * 2**20
        ),
        name="butterfly",
    )(coeffs, transfers)


def solution(mesh):
    return jax.shard_map(
        on_device,
        mesh=mesh,
        in_specs=(P("bfly", None, None), P("bfly", None, None, None, None)),
        out_specs=P("bfly", None, None),
        check_vma=False,
    )
```

```python
import functools

import jax
import jax.numpy as jnp
from jax import lax
from jax.experimental import pallas as pl
from jax.experimental.pallas import tpu as pltpu
from jax.sharding import PartitionSpec as P

LANES = 128
CHUNK = 64
RAMP = (32, 32, 32, 32,)
TAIL = (32, 32, 32, 32,)
DUE = (0.00, 3.90, 11.33, 18.92, 26.21, 35.99, 38.56, 47.12, 57.99)
PACE = 0.0710
AHEAD = 0.0700
TURN = 4
GROUP = 9
PREPARE_AFTER = 4
PREPARE_EARLY = {1: (0, 0), 2: (1, 1), 3: (1, 2), 4: (2, 1)}
LEAD = 0.00


def chunk_runs(cols):
    body = cols - sum(RAMP) - sum(TAIL)
    sizes = (CHUNK,) * (cols // CHUNK)
    if body > 0 and body % CHUNK == 0:
        sizes = RAMP + (CHUNK,) * (body // CHUNK) + TAIL
    runs = []
    for k, size in enumerate(sizes):
        if not runs or runs[-1][2] != size:
            runs.append((k, sum(sizes[:k]), size))
    return runs, sizes


def task_order(sizes, levels):
    dues = [DUE[i] if i < len(DUE) else DUE[-1] + 6.0 * (i - len(DUE) + 1) for i in range(levels + 1)]
    firsts = [sum(sizes[:k]) for k in range(len(sizes))]
    steps = [
        (firsts[k] * (AHEAD if level < TURN else PACE) + dues[level] - (LEAD if k == 0 else 0.0), -level, level, k)
        for k in range(len(sizes)) for level in range(levels + 1)
    ]
    order, turned = [], {0}
    for _, _, level, k in sorted(steps):
        block = firsts[k] // LANES
        if level == 0 and block not in turned:
            turned.add(block)
            order.append((levels + 2, block))
        order.append((level, k))
    for level in range(1, levels):
        after, k = PREPARE_EARLY.get(level, (level - 1, PREPARE_AFTER))
        at = order.index((after, min(k, len(sizes) - 1)))
        order.insert(min(at + 1, order.index((level, 0))), (levels + 1, level))
    return order


def modulo(x, n):
    return lax.bitwise_and(x, jnp.int32(n - 1)) if n & (n - 1) == 0 else lax.rem(x, jnp.int32(n))


def ring_size(order, sizes, levels):
    place = {task: i for i, task in enumerate(order)}
    for ring in range(1, len(sizes)):
        if all(
            any(
                place[level + 1, k] < place[level, j] and place[level + 1, j] < place[level, k + ring]
                for j in range(len(sizes))
            )
            for level in range(levels) for k in range(len(sizes) - ring)
        ):
            return 8 if ring in (5, 6, 7) else ring
    return len(sizes)


def kernel(axis, bits, levels, coeffs, transfers, out, own, sent, got, raw, mats, turn,
           in_sem, raw_sem, send_sem, recv_sem):
    me = lax.axis_index(axis)
    cols, rank = own.shape
    blocks = cols // LANES
    runs, sizes = chunk_runs(cols)
    order = task_order(sizes, levels)
    ring = ring_size(order, sizes, levels)

    def peer(level):
        bit = jnp.int32(level)
        for _ in range((levels - 1) // bits):
            bit = jnp.where(bit >= bits, bit - bits, bit)
        return lax.bitwise_xor(me, lax.shift_left(jnp.int32(1), bit))

    def lanes(b):
        return pl.ds(pl.multiple_of(b * LANES, LANES), LANES)

    def load_columns(first, count, sem):
        columns = (slice(None), pl.ds(first, count))
        return pltpu.make_async_copy(coeffs.at[(0, *columns)], turn.at[columns], in_sem.at[sem])

    def load_side(side):
        return pltpu.make_async_copy(transfers.at[0, 0, side], raw.at[0, side], raw_sem.at[side])

    def load_levels(first, count, sem):
        those = pl.ds(first, count)
        return pltpu.make_async_copy(transfers.at[0, those], raw.at[those], raw_sem.at[sem])

    loads = [load_columns(0, LANES, 0)]
    if blocks > 1:
        loads.append(load_columns(LANES, cols - LANES, 1))
    later = [load_levels(1, 1, 2), load_levels(2, levels - 2, 3)]

    def exchange(level, k, rows):
        return pltpu.make_async_remote_copy(
            src_ref=sent.at[level, rows],
            dst_ref=got.at[level + 1, rows],
            send_sem=send_sem.at[0],
            recv_sem=recv_sem.at[level * ring + modulo(k, ring)],
            device_id=(peer(level),),
            device_id_type=pl.DeviceIdType.MESH,
        )

    barrier = pltpu.get_barrier_semaphore()
    for bit in range(min(bits, levels)):
        pl.semaphore_signal(barrier, inc=1, device_id=(peer(bit),),
                            device_id_type=pl.DeviceIdType.MESH)

    load_side(1).start()
    loads[0].start()
    load_side(0).start()
    later[0].start()
    for load in loads[1:]:
        load.start()
    later[1].start()

    def prepare_side(level, side):
        full = raw[level, side].T
        high = full.astype(jnp.bfloat16)
        low = (full - high.astype(jnp.float32)).astype(jnp.bfloat16)
        mats[level, 0:rank, side * rank:(side + 1) * rank] = high
        mats[level, rank:2 * rank, side * rank:(side + 1) * rank] = low

    def prepare(level):
        for n, load in enumerate(later):
            @pl.when(level == n + 1)
            def _():
                load.wait()

        for side in range(2):
            prepare_side(level, side)

    def turn_block(b):
        rows = pl.ds(pl.multiple_of(b * LANES, LANES), LANES)
        own[rows] = turn[:, rows].T
        got[0, rows] = jnp.zeros((LANES, rank), jnp.float32)

    def products(state, level):
        size = state.shape[0]
        high = state.astype(jnp.bfloat16)
        low = (state - high.astype(jnp.float32)).astype(jnp.bfloat16)
        stack = jnp.concatenate([high, low], axis=0)

        def terms(first, count):
            columns = slice(first * rank, (first + count) * rank)
            both = jnp.dot(stack, mats[level, 0:rank, columns], preferred_element_type=jnp.float32)
            rest = jnp.dot(high, mats[level, rank:2 * rank, columns], preferred_element_type=jnp.float32)
            return both[:size] + both[size:] + rest

        return terms

    def apply(size, level, k, row):
        rows = pl.ds(pl.multiple_of(row, 16), size)

        @pl.when(level > 0)
        def _():
            exchange(level - 1, k, rows).wait_recv()

        terms = products(own[rows] + got[level, rows], level)
        def together():
            both = terms(0, 2)
            sent[level, rows] = both[:, rank:]
            exchange(level, k, rows).start()
            own[rows] = both[:, :rank]

        def apart():
            sent[level, rows] = terms(1, 1)
            exchange(level, k, rows).start()
            own[rows] = terms(0, 1)

        if size in (sizes[0], sizes[-1]):
            pl.when((k == 0) | (k == len(sizes) - 1))(apart)
            pl.when((k > 0) & (k < len(sizes) - 1))(together)
        else:
            together()

    def finish(size, k, row):
        rows = pl.ds(pl.multiple_of(row, 16), size)
        exchange(levels - 1, k, rows).wait_recv()
        own[rows] = own[rows] + got[levels, rows]

        @pl.when(lax.rem(row + size, LANES) == 0)
        def _():
            b = lax.div(row, LANES)
            out[0, :, lanes(b)] = own[pl.ds(pl.multiple_of(b * LANES, LANES), LANES)].T

    load_side(1).wait()
    prepare_side(0, 1)
    loads[0].wait()
    turn_block(0)
    pl.semaphore_wait(barrier, min(bits, levels))

    rows = pl.ds(0, sizes[0])
    terms = products(own[rows], 0)
    sent[0, rows] = terms(1, 1)
    exchange(jnp.int32(0), jnp.int32(0), rows).start()
    load_side(0).wait()
    prepare_side(0, 0)
    own[rows] = terms(0, 1)

    width = max(levels + 2, len(sizes) - 1).bit_length()
    pack = 31 // (2 * width)
    digits = [(level << width) + k for level, k in order if (level, k) != (0, 0)]
    words = [
        sum(d << (2 * width * i) for i, d in enumerate(digits[n:n + pack]))
        for n in range(0, len(digits), pack)
    ]
    per = GROUP // pack
    groups = pl.cdiv(len(words), per)
    words += [0] * (groups * per - len(words))

    def group(g, carry):
        held = []
        for n in range(per):
            word = jnp.int32(words[n])
            for other in range(1, groups):
                word = jnp.where(g == other, jnp.int32(words[other * per + n]), word)
            held.append(word)

        def step(j, carry):
            word = held[0]
            for n in range(1, per):
                word = jnp.where(j >= n * pack, held[n], word)
            place = j
            for n in range(1, per):
                place = jnp.where(j >= n * pack, j - n * pack, place)
            word = lax.shift_right_logical(word, place * (2 * width))
            level = lax.bitwise_and(lax.shift_right_logical(word, jnp.int32(width)), jnp.int32(2**width - 1))
            k = lax.bitwise_and(word, jnp.int32(2**width - 1))
            row = jnp.int32(0)
            for first, column, size in runs:
                row = jnp.where(k >= first, column + (k - first) * size, row)

            def by_size(act):
                for size in sorted(set(sizes)):
                    among = False
                    for (first, _, its), last in zip(runs, [r[0] for r in runs[1:]] + [len(sizes)]):
                        if its == size:
                            among = among | ((k >= first) & (k < last))

                    @pl.when(among)
                    def _():
                        act(size)

            @pl.when(level < levels)
            def _():
                by_size(lambda size: apply(size, level, k, row))

            @pl.when(level == levels)
            def _():
                by_size(lambda size: finish(size, k, row))

            @pl.when(level == levels + 1)
            def _():
                prepare(k)

            @pl.when(level == levels + 2)
            def _():
                @pl.when(k == 1)
                def _():
                    loads[1].wait()

                turn_block(k)
            return carry

        count = jnp.minimum(per * pack, len(digits) - g * per * pack)
        return lax.fori_loop(0, count, step, carry)

    lax.fori_loop(0, groups, group, 0)

    pltpu.make_async_remote_copy(
        src_ref=sent, dst_ref=got.at[pl.ds(1, levels)], send_sem=send_sem.at[0], recv_sem=recv_sem.at[0],
        device_id=(peer(0),), device_id_type=pl.DeviceIdType.MESH,
    ).wait_send()


def on_device(coeffs, transfers):
    bits = lax.axis_size("bfly").bit_length() - 1
    _, rank, cols = coeffs.shape
    levels = transfers.shape[1]
    _, sizes = chunk_runs(cols)
    f32, bf16 = jnp.float32, jnp.bfloat16
    return pl.pallas_call(
        functools.partial(kernel, "bfly", bits, levels),
        out_shape=pltpu.VMEM(coeffs.shape, f32),
        in_specs=[pl.BlockSpec(memory_space=pl.ANY)] * 2,
        out_specs=pl.BlockSpec(memory_space=pltpu.VMEM),
        scratch_shapes=[
            pltpu.VMEM((cols, rank), f32),
            pltpu.VMEM((levels, cols, rank), f32),
            pltpu.VMEM((levels + 1, cols, rank), f32),
            pltpu.VMEM((levels, 2, rank, rank), f32),
            pltpu.VMEM((levels, 2 * rank, 2 * rank), bf16),
            pltpu.VMEM((rank, cols), f32),
            pltpu.SemaphoreType.DMA((2,)),
            pltpu.SemaphoreType.DMA((4,)),
            pltpu.SemaphoreType.DMA((1,)),
            pltpu.SemaphoreType.DMA((levels * ring_size(task_order(sizes, levels), sizes, levels),)),
        ],
        compiler_params=pltpu.CompilerParams(
            collective_id=0, has_side_effects=True, vmem_limit_bytes=52 * 2**20
        ),
        name="butterfly",
    )(coeffs, transfers)


def solution(mesh):
    return jax.shard_map(
        on_device,
        mesh=mesh,
        in_specs=(P("bfly", None, None), P("bfly", None, None, None, None)),
        out_specs=P("bfly", None, None),
        check_vma=False,
    )
```

```python
import functools

import jax
import jax.numpy as jnp
from jax import lax
from jax.experimental import pallas as pl
from jax.experimental.pallas import tpu as pltpu
from jax.sharding import PartitionSpec as P

LANES = 128
CHUNK = 64
RAMP = (32, 32, 32, 32,)
TAIL = (32, 32, 32, 32,)
DUE = (0.00, 3.90, 11.33, 18.92, 26.21, 35.99, 38.56, 47.12, 57.99)
PACE = 0.0710
AHEAD = 0.0700
TURN = 4
GROUP = 9
PREPARE_AFTER = 2
PREPARE_EARLY = {1: (0, 0), 2: (1, 1), 3: (1, 2), 4: (2, 1)}
LEAD = 0.00


def chunk_runs(cols):
    body = cols - sum(RAMP) - sum(TAIL)
    sizes = (CHUNK,) * (cols // CHUNK)
    if body > 0 and body % CHUNK == 0:
        sizes = RAMP + (CHUNK,) * (body // CHUNK) + TAIL
    runs = []
    for k, size in enumerate(sizes):
        if not runs or runs[-1][2] != size:
            runs.append((k, sum(sizes[:k]), size))
    return runs, sizes


def task_order(sizes, levels):
    dues = [DUE[i] if i < len(DUE) else DUE[-1] + 6.0 * (i - len(DUE) + 1) for i in range(levels + 1)]
    firsts = [sum(sizes[:k]) for k in range(len(sizes))]
    steps = [
        (firsts[k] * (AHEAD if level < TURN else PACE) + dues[level] - (LEAD if k == 0 else 0.0), -level, level, k)
        for k in range(len(sizes)) for level in range(levels + 1)
    ]
    order, turned = [], {0}
    for _, _, level, k in sorted(steps):
        block = firsts[k] // LANES
        if level == 0 and block not in turned:
            turned.add(block)
            order.append((levels + 2, block))
        order.append((level, k))
    for level in range(1, levels):
        after, k = PREPARE_EARLY.get(level, (level - 1, PREPARE_AFTER))
        at = order.index((after, min(k, len(sizes) - 1)))
        order.insert(min(at + 1, order.index((level, 0))), (levels + 1, level))
    return order


def modulo(x, n):
    return lax.bitwise_and(x, jnp.int32(n - 1)) if n & (n - 1) == 0 else lax.rem(x, jnp.int32(n))


def ring_size(order, sizes, levels):
    place = {task: i for i, task in enumerate(order)}
    for ring in range(1, len(sizes)):
        if all(
            any(
                place[level + 1, k] < place[level, j] and place[level + 1, j] < place[level, k + ring]
                for j in range(len(sizes))
            )
            for level in range(levels) for k in range(len(sizes) - ring)
        ):
            return 8 if ring in (5, 6, 7) else ring
    return len(sizes)


def kernel(axis, bits, levels, coeffs, transfers, out, own, sent, got, raw, mats, turn,
           in_sem, raw_sem, send_sem, recv_sem):
    me = lax.axis_index(axis)
    cols, rank = own.shape
    blocks = cols // LANES
    runs, sizes = chunk_runs(cols)
    order = task_order(sizes, levels)
    ring = ring_size(order, sizes, levels)

    def peer(level):
        bit = jnp.int32(level)
        for _ in range((levels - 1) // bits):
            bit = jnp.where(bit >= bits, bit - bits, bit)
        return lax.bitwise_xor(me, lax.shift_left(jnp.int32(1), bit))

    def lanes(b):
        return pl.ds(pl.multiple_of(b * LANES, LANES), LANES)

    def load_columns(first, count, sem):
        columns = (slice(None), pl.ds(first, count))
        return pltpu.make_async_copy(coeffs.at[(0, *columns)], turn.at[columns], in_sem.at[sem])

    def load_side(side):
        return pltpu.make_async_copy(transfers.at[0, 0, side], raw.at[0, side], raw_sem.at[side])

    def load_levels(first, count, sem):
        those = pl.ds(first, count)
        return pltpu.make_async_copy(transfers.at[0, those], raw.at[those], raw_sem.at[sem])

    loads = [load_columns(0, LANES, 0)]
    if blocks > 1:
        loads.append(load_columns(LANES, cols - LANES, 1))
    later = [load_levels(1, 1, 2), load_levels(2, levels - 2, 3)]

    def exchange(level, k, rows):
        return pltpu.make_async_remote_copy(
            src_ref=sent.at[level, rows],
            dst_ref=got.at[level + 1, rows],
            send_sem=send_sem.at[0],
            recv_sem=recv_sem.at[level * ring + modulo(k, ring)],
            device_id=(peer(level),),
            device_id_type=pl.DeviceIdType.MESH,
        )

    barrier = pltpu.get_barrier_semaphore()
    for bit in range(min(bits, levels)):
        pl.semaphore_signal(barrier, inc=1, device_id=(peer(bit),),
                            device_id_type=pl.DeviceIdType.MESH)

    load_side(1).start()
    loads[0].start()
    load_side(0).start()
    later[0].start()
    for load in loads[1:]:
        load.start()
    later[1].start()

    def prepare_side(level, side):
        full = raw[level, side].T
        high = full.astype(jnp.bfloat16)
        low = (full - high.astype(jnp.float32)).astype(jnp.bfloat16)
        mats[level, 0:rank, side * rank:(side + 1) * rank] = high
        mats[level, rank:2 * rank, side * rank:(side + 1) * rank] = low

    def prepare(level):
        for n, load in enumerate(later):
            @pl.when(level == n + 1)
            def _():
                load.wait()

        for side in range(2):
            prepare_side(level, side)

    def turn_block(b):
        rows = pl.ds(pl.multiple_of(b * LANES, LANES), LANES)
        own[rows] = turn[:, rows].T
        got[0, rows] = jnp.zeros((LANES, rank), jnp.float32)

    def products(state, level):
        size = state.shape[0]
        high = state.astype(jnp.bfloat16)
        low = (state - high.astype(jnp.float32)).astype(jnp.bfloat16)
        stack = jnp.concatenate([high, low], axis=0)

        def terms(first, count):
            columns = slice(first * rank, (first + count) * rank)
            both = jnp.dot(stack, mats[level, 0:rank, columns], preferred_element_type=jnp.float32)
            rest = jnp.dot(high, mats[level, rank:2 * rank, columns], preferred_element_type=jnp.float32)
            return both[:size] + both[size:] + rest

        return terms

    def apply(size, level, k, row):
        rows = pl.ds(pl.multiple_of(row, 16), size)

        @pl.when(level > 0)
        def _():
            exchange(level - 1, k, rows).wait_recv()

        terms = products(own[rows] + got[level, rows], level)
        def together():
            both = terms(0, 2)
            sent[level, rows] = both[:, rank:]
            exchange(level, k, rows).start()
            own[rows] = both[:, :rank]

        def apart():
            sent[level, rows] = terms(1, 1)
            exchange(level, k, rows).start()
            own[rows] = terms(0, 1)

        if size in (sizes[0], sizes[-1]):
            pl.when((k == 0) | (k == len(sizes) - 1))(apart)
            pl.when((k > 0) & (k < len(sizes) - 1))(together)
        else:
            together()

    def finish(size, k, row):
        rows = pl.ds(pl.multiple_of(row, 16), size)
        exchange(levels - 1, k, rows).wait_recv()
        own[rows] = own[rows] + got[levels, rows]

        @pl.when(lax.rem(row + size, LANES) == 0)
        def _():
            b = lax.div(row, LANES)
            out[0, :, lanes(b)] = own[pl.ds(pl.multiple_of(b * LANES, LANES), LANES)].T

    load_side(1).wait()
    prepare_side(0, 1)
    loads[0].wait()
    turn_block(0)
    pl.semaphore_wait(barrier, min(bits, levels))

    rows = pl.ds(0, sizes[0])
    terms = products(own[rows], 0)
    sent[0, rows] = terms(1, 1)
    exchange(jnp.int32(0), jnp.int32(0), rows).start()
    load_side(0).wait()
    prepare_side(0, 0)
    own[rows] = terms(0, 1)

    width = max(levels + 2, len(sizes) - 1).bit_length()
    pack = 31 // (2 * width)
    digits = [(level << width) + k for level, k in order if (level, k) != (0, 0)]
    words = [
        sum(d << (2 * width * i) for i, d in enumerate(digits[n:n + pack]))
        for n in range(0, len(digits), pack)
    ]
    per = GROUP // pack
    groups = pl.cdiv(len(words), per)
    words += [0] * (groups * per - len(words))

    def group(g, carry):
        held = []
        for n in range(per):
            word = jnp.int32(words[n])
            for other in range(1, groups):
                word = jnp.where(g == other, jnp.int32(words[other * per + n]), word)
            held.append(word)

        def step(j, carry):
            word = held[0]
            for n in range(1, per):
                word = jnp.where(j >= n * pack, held[n], word)
            place = j
            for n in range(1, per):
                place = jnp.where(j >= n * pack, j - n * pack, place)
            word = lax.shift_right_logical(word, place * (2 * width))
            level = lax.bitwise_and(lax.shift_right_logical(word, jnp.int32(width)), jnp.int32(2**width - 1))
            k = lax.bitwise_and(word, jnp.int32(2**width - 1))
            row = jnp.int32(0)
            for first, column, size in runs:
                row = jnp.where(k >= first, column + (k - first) * size, row)

            def by_size(act):
                for size in sorted(set(sizes)):
                    among = False
                    for (first, _, its), last in zip(runs, [r[0] for r in runs[1:]] + [len(sizes)]):
                        if its == size:
                            among = among | ((k >= first) & (k < last))

                    @pl.when(among)
                    def _():
                        act(size)

            @pl.when(level < levels)
            def _():
                by_size(lambda size: apply(size, level, k, row))

            @pl.when(level == levels)
            def _():
                by_size(lambda size: finish(size, k, row))

            @pl.when(level == levels + 1)
            def _():
                prepare(k)

            @pl.when(level == levels + 2)
            def _():
                @pl.when(k == 1)
                def _():
                    loads[1].wait()

                turn_block(k)
            return carry

        count = jnp.minimum(per * pack, len(digits) - g * per * pack)
        return lax.fori_loop(0, count, step, carry)

    lax.fori_loop(0, groups, group, 0)

    pltpu.make_async_remote_copy(
        src_ref=sent, dst_ref=got.at[pl.ds(1, levels)], send_sem=send_sem.at[0], recv_sem=recv_sem.at[0],
        device_id=(peer(0),), device_id_type=pl.DeviceIdType.MESH,
    ).wait_send()


def on_device(coeffs, transfers):
    bits = lax.axis_size("bfly").bit_length() - 1
    _, rank, cols = coeffs.shape
    levels = transfers.shape[1]
    _, sizes = chunk_runs(cols)
    f32, bf16 = jnp.float32, jnp.bfloat16
    return pl.pallas_call(
        functools.partial(kernel, "bfly", bits, levels),
        out_shape=pltpu.VMEM(coeffs.shape, f32),
        in_specs=[pl.BlockSpec(memory_space=pl.ANY)] * 2,
        out_specs=pl.BlockSpec(memory_space=pltpu.VMEM),
        scratch_shapes=[
            pltpu.VMEM((cols, rank), f32),
            pltpu.VMEM((levels, cols, rank), f32),
            pltpu.VMEM((levels + 1, cols, rank), f32),
            pltpu.VMEM((levels, 2, rank, rank), f32),
            pltpu.VMEM((levels, 2 * rank, 2 * rank), bf16),
            pltpu.VMEM((rank, cols), f32),
            pltpu.SemaphoreType.DMA((2,)),
            pltpu.SemaphoreType.DMA((4,)),
            pltpu.SemaphoreType.DMA((1,)),
            pltpu.SemaphoreType.DMA((levels * ring_size(task_order(sizes, levels), sizes, levels),)),
        ],
        compiler_params=pltpu.CompilerParams(
            collective_id=0, has_side_effects=True, vmem_limit_bytes=52 * 2**20
        ),
        name="butterfly",
    )(coeffs, transfers)


def solution(mesh):
    return jax.shard_map(
        on_device,
        mesh=mesh,
        in_specs=(P("bfly", None, None), P("bfly", None, None, None, None)),
        out_specs=P("bfly", None, None),
        check_vma=False,
    )
```

```python
import functools

import jax
import jax.numpy as jnp
from jax import lax
from jax.experimental import pallas as pl
from jax.experimental.pallas import tpu as pltpu
from jax.sharding import PartitionSpec as P

LANES = 128
CHUNK = 64
RAMP = (32, 32, 32, 32,)
TAIL = (32, 32, 32, 32,)
DUE = (0.00, 3.90, 11.33, 18.92, 26.21, 35.99, 38.56, 47.12, 57.99)
PACE = 0.0710
AHEAD = 0.0700
TURN = 4
GROUP = 9
PREPARE_AFTER = 2
PREPARE_EARLY = {1: (0, 0), 2: (1, 1), 3: (1, 2), 4: (2, 2)}
LEAD = 0.00


def chunk_runs(cols):
    body = cols - sum(RAMP) - sum(TAIL)
    sizes = (CHUNK,) * (cols // CHUNK)
    if body > 0 and body % CHUNK == 0:
        sizes = RAMP + (CHUNK,) * (body // CHUNK) + TAIL
    runs = []
    for k, size in enumerate(sizes):
        if not runs or runs[-1][2] != size:
            runs.append((k, sum(sizes[:k]), size))
    return runs, sizes


def task_order(sizes, levels):
    dues = [DUE[i] if i < len(DUE) else DUE[-1] + 6.0 * (i - len(DUE) + 1) for i in range(levels + 1)]
    firsts = [sum(sizes[:k]) for k in range(len(sizes))]
    steps = [
        (firsts[k] * (AHEAD if level < TURN else PACE) + dues[level] - (LEAD if k == 0 else 0.0), -level, level, k)
        for k in range(len(sizes)) for level in range(levels + 1)
    ]
    order, turned = [], {0}
    for _, _, level, k in sorted(steps):
        block = firsts[k] // LANES
        if level == 0 and block not in turned:
            turned.add(block)
            order.append((levels + 2, block))
        order.append((level, k))
    for level in range(1, levels):
        after, k = PREPARE_EARLY.get(level, (level - 1, PREPARE_AFTER))
        at = order.index((after, min(k, len(sizes) - 1)))
        order.insert(min(at + 1, order.index((level, 0))), (levels + 1, level))
    return order


def modulo(x, n):
    return lax.bitwise_and(x, jnp.int32(n - 1)) if n & (n - 1) == 0 else lax.rem(x, jnp.int32(n))


def ring_size(order, sizes, levels):
    place = {task: i for i, task in enumerate(order)}
    for ring in range(1, len(sizes)):
        if all(
            any(
                place[level + 1, k] < place[level, j] and place[level + 1, j] < place[level, k + ring]
                for j in range(len(sizes))
            )
            for level in range(levels) for k in range(len(sizes) - ring)
        ):
            return 8 if ring in (5, 6, 7) else ring
    return len(sizes)


def kernel(axis, bits, levels, coeffs, transfers, out, own, sent, got, raw, mats, turn,
           in_sem, raw_sem, send_sem, recv_sem):
    me = lax.axis_index(axis)
    cols, rank = own.shape
    blocks = cols // LANES
    runs, sizes = chunk_runs(cols)
    order = task_order(sizes, levels)
    ring = ring_size(order, sizes, levels)

    def peer(level):
        bit = jnp.int32(level)
        for _ in range((levels - 1) // bits):
            bit = jnp.where(bit >= bits, bit - bits, bit)
        return lax.bitwise_xor(me, lax.shift_left(jnp.int32(1), bit))

    def lanes(b):
        return pl.ds(pl.multiple_of(b * LANES, LANES), LANES)

    def load_columns(first, count, sem):
        columns = (slice(None), pl.ds(first, count))
        return pltpu.make_async_copy(coeffs.at[(0, *columns)], turn.at[columns], in_sem.at[sem])

    def load_side(side):
        return pltpu.make_async_copy(transfers.at[0, 0, side], raw.at[0, side], raw_sem.at[side])

    def load_levels(first, count, sem):
        those = pl.ds(first, count)
        return pltpu.make_async_copy(transfers.at[0, those], raw.at[those], raw_sem.at[sem])

    loads = [load_columns(0, LANES, 0)]
    if blocks > 1:
        loads.append(load_columns(LANES, cols - LANES, 1))
    later = [load_levels(1, 1, 2), load_levels(2, levels - 2, 3)]

    def exchange(level, k, rows):
        return pltpu.make_async_remote_copy(
            src_ref=sent.at[level, rows],
            dst_ref=got.at[level + 1, rows],
            send_sem=send_sem.at[0],
            recv_sem=recv_sem.at[level * ring + modulo(k, ring)],
            device_id=(peer(level),),
            device_id_type=pl.DeviceIdType.MESH,
        )

    barrier = pltpu.get_barrier_semaphore()
    for bit in range(min(bits, levels)):
        pl.semaphore_signal(barrier, inc=1, device_id=(peer(bit),),
                            device_id_type=pl.DeviceIdType.MESH)

    load_side(1).start()
    loads[0].start()
    load_side(0).start()
    later[0].start()
    for load in loads[1:]:
        load.start()
    later[1].start()

    def prepare_side(level, side):
        full = raw[level, side].T
        high = full.astype(jnp.bfloat16)
        low = (full - high.astype(jnp.float32)).astype(jnp.bfloat16)
        mats[level, 0:rank, side * rank:(side + 1) * rank] = high
        mats[level, rank:2 * rank, side * rank:(side + 1) * rank] = low

    def prepare(level):
        for n, load in enumerate(later):
            @pl.when(level == n + 1)
            def _():
                load.wait()

        for side in range(2):
            prepare_side(level, side)

    def turn_block(b):
        rows = pl.ds(pl.multiple_of(b * LANES, LANES), LANES)
        own[rows] = turn[:, rows].T
        got[0, rows] = jnp.zeros((LANES, rank), jnp.float32)

    def products(state, level):
        size = state.shape[0]
        high = state.astype(jnp.bfloat16)
        low = (state - high.astype(jnp.float32)).astype(jnp.bfloat16)
        stack = jnp.concatenate([high, low], axis=0)

        def terms(first, count):
            columns = slice(first * rank, (first + count) * rank)
            both = jnp.dot(stack, mats[level, 0:rank, columns], preferred_element_type=jnp.float32)
            rest = jnp.dot(high, mats[level, rank:2 * rank, columns], preferred_element_type=jnp.float32)
            return both[:size] + both[size:] + rest

        return terms

    def apply(size, level, k, row):
        rows = pl.ds(pl.multiple_of(row, 16), size)

        @pl.when(level > 0)
        def _():
            exchange(level - 1, k, rows).wait_recv()

        terms = products(own[rows] + got[level, rows], level)
        def together():
            both = terms(0, 2)
            sent[level, rows] = both[:, rank:]
            exchange(level, k, rows).start()
            own[rows] = both[:, :rank]

        def apart():
            sent[level, rows] = terms(1, 1)
            exchange(level, k, rows).start()
            own[rows] = terms(0, 1)

        if size in (sizes[0], sizes[-1]):
            pl.when((k == 0) | (k == len(sizes) - 1))(apart)
            pl.when((k > 0) & (k < len(sizes) - 1))(together)
        else:
            together()

    def finish(size, k, row):
        rows = pl.ds(pl.multiple_of(row, 16), size)
        exchange(levels - 1, k, rows).wait_recv()
        own[rows] = own[rows] + got[levels, rows]

        @pl.when(lax.rem(row + size, LANES) == 0)
        def _():
            b = lax.div(row, LANES)
            out[0, :, lanes(b)] = own[pl.ds(pl.multiple_of(b * LANES, LANES), LANES)].T

    load_side(1).wait()
    prepare_side(0, 1)
    loads[0].wait()
    turn_block(0)
    pl.semaphore_wait(barrier, min(bits, levels))

    rows = pl.ds(0, sizes[0])
    terms = products(own[rows], 0)
    sent[0, rows] = terms(1, 1)
    exchange(jnp.int32(0), jnp.int32(0), rows).start()
    load_side(0).wait()
    prepare_side(0, 0)
    own[rows] = terms(0, 1)

    width = max(levels + 2, len(sizes) - 1).bit_length()
    pack = 31 // (2 * width)
    digits = [(level << width) + k for level, k in order if (level, k) != (0, 0)]
    words = [
        sum(d << (2 * width * i) for i, d in enumerate(digits[n:n + pack]))
        for n in range(0, len(digits), pack)
    ]
    per = GROUP // pack
    groups = pl.cdiv(len(words), per)
    words += [0] * (groups * per - len(words))

    def group(g, carry):
        held = []
        for n in range(per):
            word = jnp.int32(words[n])
            for other in range(1, groups):
                word = jnp.where(g == other, jnp.int32(words[other * per + n]), word)
            held.append(word)

        def step(j, carry):
            word = held[0]
            for n in range(1, per):
                word = jnp.where(j >= n * pack, held[n], word)
            place = j
            for n in range(1, per):
                place = jnp.where(j >= n * pack, j - n * pack, place)
            word = lax.shift_right_logical(word, place * (2 * width))
            level = lax.bitwise_and(lax.shift_right_logical(word, jnp.int32(width)), jnp.int32(2**width - 1))
            k = lax.bitwise_and(word, jnp.int32(2**width - 1))
            row = jnp.int32(0)
            for first, column, size in runs:
                row = jnp.where(k >= first, column + (k - first) * size, row)

            def by_size(act):
                for size in sorted(set(sizes)):
                    among = False
                    for (first, _, its), last in zip(runs, [r[0] for r in runs[1:]] + [len(sizes)]):
                        if its == size:
                            among = among | ((k >= first) & (k < last))

                    @pl.when(among)
                    def _():
                        act(size)

            @pl.when(level < levels)
            def _():
                by_size(lambda size: apply(size, level, k, row))

            @pl.when(level == levels)
            def _():
                by_size(lambda size: finish(size, k, row))

            @pl.when(level == levels + 1)
            def _():
                prepare(k)

            @pl.when(level == levels + 2)
            def _():
                @pl.when(k == 1)
                def _():
                    loads[1].wait()

                turn_block(k)
            return carry

        count = jnp.minimum(per * pack, len(digits) - g * per * pack)
        return lax.fori_loop(0, count, step, carry)

    lax.fori_loop(0, groups, group, 0)

    pltpu.make_async_remote_copy(
        src_ref=sent, dst_ref=got.at[pl.ds(1, levels)], send_sem=send_sem.at[0], recv_sem=recv_sem.at[0],
        device_id=(peer(0),), device_id_type=pl.DeviceIdType.MESH,
    ).wait_send()


def on_device(coeffs, transfers):
    bits = lax.axis_size("bfly").bit_length() - 1
    _, rank, cols = coeffs.shape
    levels = transfers.shape[1]
    _, sizes = chunk_runs(cols)
    f32, bf16 = jnp.float32, jnp.bfloat16
    return pl.pallas_call(
        functools.partial(kernel, "bfly", bits, levels),
        out_shape=pltpu.VMEM(coeffs.shape, f32),
        in_specs=[pl.BlockSpec(memory_space=pl.ANY)] * 2,
        out_specs=pl.BlockSpec(memory_space=pltpu.VMEM),
        scratch_shapes=[
            pltpu.VMEM((cols, rank), f32),
            pltpu.VMEM((levels, cols, rank), f32),
            pltpu.VMEM((levels + 1, cols, rank), f32),
            pltpu.VMEM((levels, 2, rank, rank), f32),
            pltpu.VMEM((levels, 2 * rank, 2 * rank), bf16),
            pltpu.VMEM((rank, cols), f32),
            pltpu.SemaphoreType.DMA((2,)),
            pltpu.SemaphoreType.DMA((4,)),
            pltpu.SemaphoreType.DMA((1,)),
            pltpu.SemaphoreType.DMA((levels * ring_size(task_order(sizes, levels), sizes, levels),)),
        ],
        compiler_params=pltpu.CompilerParams(
            collective_id=0, has_side_effects=True, vmem_limit_bytes=52 * 2**20
        ),
        name="butterfly",
    )(coeffs, transfers)


def solution(mesh):
    return jax.shard_map(
        on_device,
        mesh=mesh,
        in_specs=(P("bfly", None, None), P("bfly", None, None, None, None)),
        out_specs=P("bfly", None, None),
        check_vma=False,
    )
```
